256 devices in a mesh: freq: 8 (over x, core), tile: 32 (over y, z).
Axes of the slice: x: 4, y: 4, z: 8, core: 2. Of those that a mesh axis runs over, the one named last changes fastest.
Arguments:
- model_field: bfloat16 [8, 16384, 256], P('freq', 'tile'), may hold values from -6 to 6
- data_field: bfloat16 [8, 16384, 256], P('freq', 'tile'), may hold values from -6 to 6
- u_codes: bfloat16 [8, 2, 16384, 2816], P('freq', None, 'tile'), may hold values from -128 to 127, as said below
- u_scales: float32 [8, 32, 2816], P('freq', 'tile'), as said below
- v_codes: bfloat16 [8, 2, 16384, 2816], P('freq', None, 'tile'), may hold values from -128 to 127, as said below
- v_scales: float32 [8, 32, 2816], P('freq', 'tile'), as said below
- tile_ranks: int32 [8, 32, 32], P('freq'), may hold values from 40 to 88, as said below
- mute_start: int32 [16384], P('tile'), may hold values from 0 to 64
Outputs:
- gradient_time: bfloat16 [16384, 128, 128], P('tile', 'freq')
The draws below stay inside these ranges and needn't reach their ends.
Inputs may be any that keep to these rules, and one draw needn't show every extreme that they name: `tile_ranks`: for every frequency the ranks are symmetric; one tile row (and column), drawn per frequency, has every tile of rank 88, so its total is exactly 2816; no row or column totals more. `u_codes`: whole numbers. `v_codes`: whole numbers. `u_scales`: Positive. `v_scales`: Positive.
All inputs are finite; a program needn't handle non-finite values.
Results may differ from the reference program's by a relative error of at most 0.0075.
Values may be sent and summed in bfloat16 or wider, within the bound.
No kernel may reach another device: no remote copies, remote signals or barrier semaphores. Data moves between devices by JAX's collectives and lax.ppermute only.
A program may use at most 128 MiB of HBM per device.

```python
import math
import jax
import jax.numpy as jnp
from jax import lax

B = 512
RSLOT = 88
RLO = 40
RHI = 80
S = 128
NTIME = 128
NT = 32
NF = 8
ORDER = 16384
CAP = 2816


def code_table(key):
    whole = jax.random.randint(key, (NF, 2, ORDER, CAP), -128, 128, dtype=jnp.int32)
    return whole.astype(jnp.float32).astype(jnp.bfloat16)


def draw_u_codes(key, part):
    return code_table(jax.random.fold_in(key, 11))


def draw_v_codes(key, part):
    return code_table(jax.random.fold_in(key, 12))


def scale_table(key, base_std):
    low_end = math.log(0.3)
    high_end = math.log(3.0)
    spread = jax.random.uniform(key, (NF, NT, CAP), jnp.float32, low_end, high_end)
    return (jnp.exp(spread) * (base_std / 73.9)).astype(jnp.float32)


def draw_u_scales(key, part):
    return scale_table(jax.random.fold_in(key, 21), 1.0 / math.sqrt(CAP))


def draw_v_scales(key, part):
    return scale_table(jax.random.fold_in(key, 22), 1.0 / math.sqrt(2 * B))


def draw_tile_ranks(key, part):
    own_key = jax.random.fold_in(key, 31)
    base_key, pick_key = jax.random.split(own_key)
    base_draw = jax.random.randint(base_key, (NF, NT, NT), RLO, RHI + 1, dtype=jnp.int32)
    symmetric = jnp.triu(base_draw) + jnp.swapaxes(jnp.triu(base_draw, 1), 1, 2)
    heavy_row = jax.random.randint(pick_key, (NF,), 0, NT, dtype=jnp.int32)
    positions = jnp.arange(NT, dtype=jnp.int32)
    is_heavy = positions[None, :] == heavy_row[:, None]
    heavy_mask = is_heavy[:, :, None] | is_heavy[:, None, :]
    return jnp.where(heavy_mask, RSLOT, symmetric).astype(jnp.int32)


def place_ends(values, rng, smallest, top_value):
    longest = values.shape.index(max(values.shape))
    spots = []
    for shift in (0, 1):
        where = [jax.random.randint(jax.random.fold_in(rng, axis), (), 0, length) for axis, length in enumerate(values.shape)]
        where[longest] = (where[longest] + shift) % values.shape[longest]
        spots.append(tuple(where))
    return values.at[spots[0]].set(smallest).at[spots[1]].set(top_value)


def shard_levels(rng, extent, pieces, low, top_value):
    loudness, own = 1.0, jax.random.fold_in(rng, 6)
    for position, blocks in pieces:
        draws = jnp.exp(jax.random.uniform(jax.random.fold_in(own, position), (blocks,), jnp.float32, low / len(pieces), top_value / len(pieces)))
        loudness = loudness * jnp.repeat(draws, extent[position] // blocks).reshape([-1 if axis == position else 1 for axis in range(len(extent))])
    return loudness


def centred(rng, shape, deviation, limit, shards=(), kind=jnp.bfloat16):
    drawn = jax.random.normal(rng, shape, jnp.float32) * deviation
    if len(shards) > 0:
        drawn = shard_levels(rng, shape, shards, -0.22, 0.18) * drawn
    return jnp.clip(drawn, min=-limit, max=limit).astype(kind)


def setup_inputs(seed: int = 0) -> dict:
    keys = jax.random.split(jax.random.key(seed), 9)
    model_field = centred(keys[0], (NF, ORDER, 2 * S), 1.0, 6.0, ((0, 8), (1, 32)))
    data_field = centred(keys[1], (NF, ORDER, 2 * S), 1.0, 6.0, ((0, 8), (1, 32)))
    u_codes = draw_u_codes(jax.random.fold_in(keys[8], 71), 0)
    u_scales = draw_u_scales(jax.random.fold_in(keys[8], 71), 0)
    v_codes = draw_v_codes(jax.random.fold_in(keys[8], 71), 0)
    v_scales = draw_v_scales(jax.random.fold_in(keys[8], 71), 0)
    tile_ranks = draw_tile_ranks(jax.random.fold_in(keys[8], 71), 0)
    mute_start = place_ends(jax.random.randint(keys[7], (ORDER,), 0, NTIME // 2 + 1), jax.random.fold_in(keys[7], 1), 0, (NTIME // 2 + 1) - 1).astype(jnp.int32)
    return {"model_field": model_field, "data_field": data_field, "u_codes": u_codes, "u_scales": u_scales, "v_codes": v_codes, "v_scales": v_scales, "tile_ranks": tile_ranks, "mute_start": mute_start}


def unpack_pool(code_vals, scale_row):
    return (code_vals.astype(jnp.float32) * scale_row).astype(jnp.bfloat16)

def apply_factor(factor, pooled):
    half_width = pooled.shape[1] // 2
    real_part = jnp.dot(factor[0], pooled, preferred_element_type=jnp.float32)
    imag_part = jnp.dot(factor[1], pooled, preferred_element_type=jnp.float32)
    out_re = real_part[:, :half_width] - imag_part[:, half_width:]
    out_im = real_part[:, half_width:] + imag_part[:, :half_width]
    return jnp.concatenate([out_re, out_im], 1)

def apply_adjoint(factor, dense_rows):
    half_width = dense_rows.shape[1] // 2
    dims = (((0,), (0,)), ((), ()))
    real_part = lax.dot_general(factor[0], dense_rows, dims, preferred_element_type=jnp.float32)
    imag_part = lax.dot_general(factor[1], dense_rows, dims, preferred_element_type=jnp.float32)
    out_re = real_part[:, :half_width] + imag_part[:, half_width:]
    out_im = real_part[:, half_width:] - imag_part[:, :half_width]
    return jnp.concatenate([out_re, out_im], 1)

def pool_owner(ends, begins, capacity, tile_count):
    column = jnp.arange(capacity, dtype=jnp.int32)
    owner_raw = lax.optimization_barrier(jnp.sum((column[:, None] >= ends[None, :]).astype(jnp.int32), 1)).astype(jnp.int32)
    is_live = owner_raw < tile_count
    owner_tile = jnp.minimum(owner_raw, tile_count - 1).astype(jnp.int32)
    offset = (column - begins[owner_tile]).astype(jnp.int32)
    return (owner_tile, offset, is_live)

def reference(model_field, data_field, u_codes, u_scales, v_codes, v_scales, tile_ranks, mute_start):
    tile_count = NT
    capacity = CAP
    src_width = S

    def one_freq(freq_idx):
        rank_table = tile_ranks[freq_idx]
        row_end = jnp.cumsum(rank_table, 1).astype(jnp.int32)
        row_begin = (row_end - rank_table).astype(jnp.int32)
        col_end = jnp.cumsum(rank_table, 0).astype(jnp.int32)
        col_begin = (col_end - rank_table).astype(jnp.int32)
        model_f = model_field[freq_idx]
        data_f = data_field[freq_idx]
        ucodes_f = u_codes[freq_idx]
        vcodes_f = v_codes[freq_idx]
        uscale_f = u_scales[freq_idx]
        vscale_f = v_scales[freq_idx]

        def right_factor(col_tile):
            return unpack_pool(lax.dynamic_slice_in_dim(vcodes_f, col_tile * B, B, 1), vscale_f[col_tile])

        def column_pool(col_tile):
            factor = right_factor(col_tile)
            local_model = lax.dynamic_slice_in_dim(model_f, col_tile * B, B, 0)
            return apply_adjoint(factor, local_model).astype(jnp.bfloat16)
        tiles = jnp.arange(tile_count, dtype=jnp.int32)
        w_pools = lax.map(column_pool, tiles).reshape(tile_count * capacity, 2 * src_width)

        def row_section(row_tile):
            owner_tile, offset, is_live = pool_owner(row_end[row_tile], row_begin[row_tile], capacity, tile_count)
            source = owner_tile * capacity + col_begin[row_tile, owner_tile] + offset
            source = jnp.where(is_live, source, 0).astype(jnp.int32)
            pooled = jnp.where(is_live[:, None], w_pools[source], 0).astype(jnp.bfloat16)
            factor = unpack_pool(lax.dynamic_slice_in_dim(ucodes_f, row_tile * B, B, 1), uscale_f[row_tile])
            local_data = lax.dynamic_slice_in_dim(data_f, row_tile * B, B, 0).astype(jnp.float32)
            residual = (apply_factor(factor, pooled) - local_data).astype(jnp.bfloat16)
            return apply_adjoint(factor, residual).astype(jnp.bfloat16)
        p_pools = lax.map(row_section, tiles).reshape(tile_count * capacity, 2 * src_width)

        def column_grad(col_tile):
            owner_tile, offset, is_live = pool_owner(col_end[:, col_tile], col_begin[:, col_tile], capacity, tile_count)
            source = owner_tile * capacity + row_begin[owner_tile, col_tile] + offset
            source = jnp.where(is_live, source, 0).astype(jnp.int32)
            pooled = jnp.where(is_live[:, None], p_pools[source], 0).astype(jnp.bfloat16)
            return apply_factor(right_factor(col_tile), pooled).astype(jnp.bfloat16)
        return lax.map(column_grad, tiles).reshape(tile_count * B, 2 * src_width)
    spectra = lax.map(one_freq, jnp.arange(NF, dtype=jnp.int32))
    spectra = spectra.reshape(NF, tile_count * B, 2, src_width).astype(jnp.float32)
    freq_bin = jnp.arange(NF, dtype=jnp.int32).astype(jnp.float32) + 1.0
    time_grid = jnp.arange(NTIME, dtype=jnp.int32).astype(jnp.float32)
    phase_arg = 2.0 * math.pi * freq_bin[:, None] * time_grid[None, :] / NTIME
    time_basis = jnp.stack([jnp.cos(phase_arg), -jnp.sin(phase_arg)], 1)
    signal = 0.5 * jnp.einsum('fncs,fct->nst', spectra, time_basis, precision=lax.Precision.HIGHEST)
    unmuted = jnp.arange(NTIME, dtype=jnp.int32)[None, None, :] >= mute_start[:, None, None]
    return jnp.where(unmuted, signal, 0.0).astype(jnp.bfloat16)
```

```python
import functools
import math

import jax
import jax.numpy as jnp
import numpy as np
from jax import lax
from jax.experimental import pallas as pl
from jax.experimental.pallas import tpu as pltpu
from jax.sharding import PartitionSpec as P

RSLOT = 88
NTIME = 128
BLK = 256
WIN = 384
F32 = jnp.float32
BF16 = jnp.bfloat16
NT_DIMS = (((1,), (1,)), ((), ()))


def time_basis(freq_count, per):
    arg = 2.0 * math.pi * (np.arange(freq_count)[:, None] + 1.0) * np.arange(NTIME)[None, :] / NTIME
    base = 0.5 * np.stack([np.cos(arg), -np.sin(arg)], 1)
    rows = np.repeat(base.reshape(freq_count * 2, NTIME), per, 0).astype(np.float32)
    high = rows.astype(jnp.bfloat16)
    low = (rows - high.astype(np.float32)).astype(jnp.bfloat16)
    return np.concatenate([high, low], 1)


def start_all(*copies):
    for copy in copies:
        copy.start()
    return copies


def coef_kernel(ranks_in, codes, scale_in, model_in, out, ranks, scale, model, plain, rotated, held, first, pool, sems):
    parts, rows, cap = codes.shape
    tiles = ranks.shape[0]
    half = model.shape[1] // 2
    mine = lax.axis_index("tile")
    small = start_all(
        pltpu.make_async_copy(model_in, model, sems.at[0]),
        pltpu.make_async_copy(scale_in, scale, sems.at[1]),
        pltpu.make_async_copy(ranks_in, ranks, sems.at[2]),
    )
    big = start_all(*[pltpu.make_async_copy(codes.at[part], held.at[part], sems.at[3 + part]) for part in range(parts)])
    for lane in range(2):
        pool[lane, cap:cap + RSLOT + 8, :] = jnp.zeros((RSLOT + 8, 128), F32)
    small[0].wait()
    turned = model[...].astype(F32).T
    plain[...] = turned.astype(BF16)
    rotated[:half] = turned[half:].astype(BF16)
    rotated[half:] = (-turned[:half]).astype(BF16)
    small[1].wait()
    small[2].wait()
    piece = cap // 2
    big[0].wait()
    for at in range(0, cap, piece):
        first[:, at:at + piece] = jnp.dot(plain[...], held[0, :, at:at + piece], preferred_element_type=F32)
    big[1].wait()
    for at in range(0, cap, piece):
        acc = first[:, at:at + piece] + jnp.dot(rotated[...], held[1, :, at:at + piece], preferred_element_type=F32)
        upright = (acc * scale[:, at:at + piece]).T
        for lane in range(2):
            pool[lane, at:at + piece, :] = upright[:, lane * 128:lane * 128 + 128]

    def move(tile, begin):
        for lane in range(2):
            out[tile, :, lane * 128:lane * 128 + 128] = pool[lane, pl.ds(begin, RSLOT), :].astype(BF16)
        return begin + ranks[tile, mine]

    lax.fori_loop(0, tiles, move, jnp.int32(0))


def in_hbm(*arrays):
    return [pltpu.with_memory_space_constraint(array, pltpu.HBM) for array in arrays]


def coef(ranks, codes, scale, model):
    parts, rows, cap = codes.shape
    width = model.shape[1]
    tiles = ranks.shape[0]
    return pl.pallas_call(
        coef_kernel,
        in_specs=[pl.BlockSpec(memory_space=pl.ANY)] * 4,
        out_specs=pl.BlockSpec(memory_space=pltpu.VMEM),
        out_shape=jax.ShapeDtypeStruct((tiles, RSLOT, width), BF16),
        scratch_shapes=[
            pltpu.SMEM(ranks.shape, jnp.int32),
            pltpu.VMEM(scale.shape, F32),
            pltpu.VMEM(model.shape, BF16),
            pltpu.VMEM((width, rows), BF16),
            pltpu.VMEM((width, rows), BF16),
            pltpu.VMEM((parts, rows, cap), BF16),
            pltpu.VMEM((width, cap), F32),
            pltpu.VMEM((2, cap + RSLOT + 8, 128), F32),
            pltpu.SemaphoreType.DMA((3 + parts,)),
        ],
        compiler_params=pltpu.CompilerParams(vmem_limit_bytes=32 << 20),
        cost_estimate=pl.CostEstimate(flops=4 * cap * rows * width, bytes_accessed=parts * rows * cap * 2, transcendentals=0),
        name="coef",
    )(*in_hbm(ranks, codes, scale, model))


def slot_kernel(by_row, with_turned, ranks, codes, scale, *rest):
    out = rest[0]
    turned = rest[1] if with_turned else None
    begin, rank = rest[-2:]
    step = pl.program_id(0)
    tiles = ranks.shape[0]
    cap = codes.shape[2]
    mine = lax.axis_index("tile")

    @pl.when(step == 0)
    def _():
        def fill(tile, acc):
            here = ranks[mine, tile] if by_row else ranks[tile, mine]
            begin[tile] = acc
            rank[tile] = here
            return acc + here

        lax.fori_loop(0, tiles, fill, jnp.int32(0))

    first_tile = (step * BLK) // RSLOT
    inside = step * BLK - first_tile * RSLOT
    first = begin[first_tile] + jnp.minimum(inside, rank[first_tile])
    start = pl.multiple_of(jnp.minimum((first // 128) * 128, cap - WIN), 128)
    lane = lax.broadcasted_iota(jnp.int32, (1, BLK), 1)
    where_from = jnp.full((1, BLK), -1, jnp.int32)
    for ahead in range(-(-BLK // RSLOT) + 1):
        tile = jnp.minimum(first_tile + ahead, tiles - 1)
        offset = lane + (step * BLK - tile * RSLOT)
        live = (offset >= 0) & (offset < rank[tile])
        where_from = jnp.where(live, offset + (begin[tile] - start), where_from)
    picks = jnp.where(lax.broadcasted_iota(jnp.int32, (WIN, BLK), 0) == where_from, 1.0, 0.0).astype(BF16)
    window = scale[:, pl.ds(start, WIN)]
    high = window.astype(BF16).astype(F32)
    middle = (window - high).astype(BF16).astype(F32)
    low = window - high - middle
    row = lax.broadcasted_iota(jnp.int32, (16, WIN), 0)
    split = jnp.where(row == 0, high, jnp.where(row == 1, middle, jnp.where(row == 2, low, 0.0))).astype(BF16)
    weight = jnp.sum(jnp.dot(split, picks, preferred_element_type=F32), 0, keepdims=True)
    rows = codes.shape[1]
    for part in range(2):
        moved = jnp.dot(codes[part, :, pl.ds(start, WIN)], picks, preferred_element_type=F32) * weight
        out[part] = moved.astype(BF16)
        if with_turned:
            turned[:, part * rows:part * rows + rows] = moved.T.astype(BF16)


def slots(by_row, with_turned, ranks, codes, scale):
    parts, rows, cap = codes.shape
    tiles = ranks.shape[0]
    out_specs = [pl.BlockSpec((parts, rows, BLK), lambda i: (0, 0, i))]
    out_shape = [jax.ShapeDtypeStruct((parts, rows, tiles * RSLOT), BF16)]
    if with_turned:
        out_specs.append(pl.BlockSpec((BLK, parts * rows), lambda i: (i, 0)))
        out_shape.append(jax.ShapeDtypeStruct((tiles * RSLOT, parts * rows), BF16))
    return pl.pallas_call(
        functools.partial(slot_kernel, by_row, with_turned),
        grid=(tiles * RSLOT // BLK,),
        in_specs=[
            pl.BlockSpec(memory_space=pltpu.SMEM),
            pl.BlockSpec((parts, rows, cap), lambda i: (0, 0, 0), pipeline_mode=pl.Buffered(1)),
            pl.BlockSpec((1, cap), lambda i: (0, 0)),
        ],
        out_specs=out_specs,
        out_shape=out_shape,
        scratch_shapes=[pltpu.SMEM((tiles,), jnp.int32), pltpu.SMEM((tiles,), jnp.int32)],
        compiler_params=pltpu.CompilerParams(vmem_limit_bytes=16 << 20),
        cost_estimate=pl.CostEstimate(flops=4 * cap * rows * WIN, bytes_accessed=2 * parts * rows * cap * 2, transcendentals=0),
        name="slot_rows" if by_row else "slot_cols",
    )(ranks, codes, scale)


def complex_rows(stacked, rows, lanes):
    half = lanes // 2
    imag = stacked[rows:]
    swapped = jnp.concatenate([imag[:, half:], imag[:, :half]], 1)
    sign = jnp.where(lax.broadcasted_iota(jnp.int32, (1, lanes), 1) < half, -1.0, 1.0)
    return stacked[:rows] + swapped * sign


def stream(source, target, sems, pieces):
    lead, rows, _ = source.shape
    step = rows // pieces
    todo = []
    for index in range(lead):
        for k in range(pieces):
            at = pl.ds(k * step, step)
            copy = pltpu.make_async_copy(source.at[index, at], target.at[index, at], sems.at[index * pieces + k])
            copy.start()
            todo.append((copy, index, k * step))
    return todo, step


def residual_kernel(coefs, factor, turned, data, out, held, held_turned, got, both, sems, more_sems):
    parts, rows, cap = factor.shape
    lanes = coefs.shape[1]
    half = lanes // 2
    todo, step = stream(factor, held, sems, sems.shape[0] // parts)
    later, later_step = stream(turned, held_turned, more_sems, more_sems.shape[0])
    for copy, part, at in todo:
        copy.wait()
        got[part * rows + at:part * rows + at + step] = jnp.dot(held[part, at:at + step], coefs[...], preferred_element_type=F32)
    predicted = complex_rows(got[...], rows, lanes)
    rest = (predicted - data[...].astype(F32)).astype(BF16).astype(F32)
    swapped = jnp.concatenate([rest[:, half:], rest[:, :half]], 1)
    sign = jnp.where(lax.broadcasted_iota(jnp.int32, (1, lanes), 1) < half, 1.0, -1.0)
    both[:rows] = rest.astype(BF16)
    both[rows:] = (swapped * sign).astype(BF16)
    for copy, _, at in later:
        copy.wait()
        out[at:at + later_step] = jnp.dot(held_turned[0, at:at + later_step], both[...], preferred_element_type=F32).astype(BF16)


def residual(coefs, factor, turned, data):
    parts, rows, cap = factor.shape
    lanes = coefs.shape[1]
    vmem, hbm = pl.BlockSpec(memory_space=pltpu.VMEM), pl.BlockSpec(memory_space=pl.ANY)
    factor, turned = in_hbm(factor, turned[None])
    return pl.pallas_call(
        residual_kernel,
        in_specs=[vmem, hbm, hbm, vmem],
        out_specs=vmem,
        out_shape=jax.ShapeDtypeStruct((cap, lanes), BF16),
        scratch_shapes=[
            pltpu.VMEM((parts, rows, cap), BF16),
            pltpu.VMEM((1, cap, parts * rows), BF16),
            pltpu.VMEM((parts * rows, lanes), F32),
            pltpu.VMEM((parts * rows, lanes), BF16),
            pltpu.SemaphoreType.DMA((2 * parts,)),
            pltpu.SemaphoreType.DMA((2,)),
        ],
        compiler_params=pltpu.CompilerParams(vmem_limit_bytes=32 << 20),
        cost_estimate=pl.CostEstimate(flops=8 * cap * rows * lanes, bytes_accessed=2 * cap * lanes * 2, transcendentals=0),
        name="residual",
    )(coefs, factor, turned, data)


def gradient_kernel(coefs, factor, out, held, got, sems):
    parts, rows, cap = factor.shape
    lanes = coefs.shape[1]
    todo, step = stream(factor, held, sems, sems.shape[0] // parts)
    for copy, part, at in todo:
        copy.wait()
        got[part * rows + at:part * rows + at + step] = jnp.dot(held[part, at:at + step], coefs[...], preferred_element_type=F32)
    flipped = complex_rows(got[...], rows, lanes).T
    owners, each, _ = out.shape
    half = each // 2
    for owner in range(owners):
        for ri in range(2):
            at = ri * (lanes // 2) + owner * half
            out[owner, ri * half:ri * half + half, :] = flipped[at:at + half].astype(BF16)


def gradient(coefs, factor, owners):
    parts, rows, cap = factor.shape
    lanes = coefs.shape[1]
    vmem = pl.BlockSpec(memory_space=pltpu.VMEM)
    return pl.pallas_call(
        gradient_kernel,
        in_specs=[vmem, pl.BlockSpec(memory_space=pl.ANY)],
        out_specs=vmem,
        out_shape=jax.ShapeDtypeStruct((owners, lanes // owners, rows), BF16),
        scratch_shapes=[
            pltpu.VMEM((parts, rows, cap), BF16),
            pltpu.VMEM((parts * rows, lanes), F32),
            pltpu.SemaphoreType.DMA((2 * parts,)),
        ],
        compiler_params=pltpu.CompilerParams(vmem_limit_bytes=20 << 20),
        cost_estimate=pl.CostEstimate(flops=4 * cap * rows * lanes, bytes_accessed=cap * lanes * 2, transcendentals=0),
        name="gradient",
    )(coefs, *in_hbm(factor))


def time_kernel(mute, arrived, basis, out, spectra):
    step = pl.program_id(0)
    here, share, times = out.shape
    depth = basis.shape[0]

    @pl.when(step == 0)
    def _():
        spectra[...] = arrived[...].reshape(depth, arrived.shape[2]).astype(F32).T

    lane = lax.broadcasted_iota(jnp.int32, (share, depth), 1)
    row = lax.broadcasted_iota(jnp.int32, (share, depth), 0)
    own = row == lane % share
    when = lax.broadcasted_iota(jnp.int32, (share, times), 1)
    base = step * here
    lines = []
    for n in range(here):
        lines.append(jnp.where(own, spectra[pl.ds(base + n, 1), :], 0.0).astype(BF16))
    got = jnp.dot(jnp.concatenate(lines, 0), basis[...], preferred_element_type=F32)
    signal = got[:, :times] + got[:, times:]
    for n in range(here):
        out[n] = jnp.where(when >= mute[base + n], signal[n * share:n * share + share], 0.0).astype(BF16)


def to_time(mute, arrived, basis, rows, share):
    block = 128
    return pl.pallas_call(
        time_kernel,
        grid=(rows // block,),
        in_specs=[
            pl.BlockSpec(memory_space=pltpu.SMEM),
            pl.BlockSpec(arrived.shape, lambda i: (0, 0, 0)),
            pl.BlockSpec(basis.shape, lambda i: (0, 0)),
        ],
        out_specs=pl.BlockSpec((block, share, NTIME), lambda i: (i, 0, 0)),
        out_shape=jax.ShapeDtypeStruct((rows, share, NTIME), BF16),
        scratch_shapes=[pltpu.VMEM((rows, basis.shape[0]), F32)],
        compiler_params=pltpu.CompilerParams(vmem_limit_bytes=16 << 20),
        name="to_time",
    )(mute, arrived, basis)


def shards(model_field, data_field, u_codes, u_scales, v_codes, v_scales, tile_ranks, mute_start):
    ranks = tile_ranks[0]
    tiles = ranks.shape[0]
    rows = model_field.shape[1]
    width = model_field.shape[2]
    freq_count = lax.axis_size("freq")
    sources = width // 2
    share = sources // freq_count
    basis = jnp.asarray(time_basis(freq_count, share))
    sent = coef(ranks, v_codes[0], v_scales[0], model_field[0])
    late_u, late_v, sent = lax.optimization_barrier((u_codes[0], v_codes[0], sent))
    arrived = lax.all_to_all(sent, "tile", split_axis=0, concat_axis=0, tiled=True)
    u_slots, u_turned = slots(True, True, ranks, late_u, u_scales[0])
    v_slots, = slots(False, False, ranks, late_v, v_scales[0])
    back = residual(arrived.reshape(tiles * RSLOT, width), u_slots, u_turned, data_field[0])
    back = lax.all_to_all(back.reshape(tiles, RSLOT, width), "tile", split_axis=0, concat_axis=0, tiled=True)
    part = gradient(back.reshape(tiles * RSLOT, width), v_slots, freq_count)
    spectra = lax.all_to_all(part, "freq", split_axis=0, concat_axis=0, tiled=True)
    return to_time(mute_start, spectra, basis, rows, share)


def solution(mesh):
    in_specs = (
        P("freq", "tile", None),
        P("freq", "tile", None),
        P("freq", None, "tile", None),
        P("freq", "tile", None),
        P("freq", None, "tile", None),
        P("freq", "tile", None),
        P("freq", None, None),
        P("tile"),
    )
    out_specs = P("tile", "freq", None)
    return jax.shard_map(shards, mesh=mesh, in_specs=in_specs, out_specs=out_specs, check_vma=False)
```

```python
import functools
import math

import jax
import jax.numpy as jnp
import numpy as np
from jax import lax
from jax.experimental import pallas as pl
from jax.experimental.pallas import tpu as pltpu
from jax.sharding import PartitionSpec as P

RSLOT = 88
NTIME = 128
BLK = 256
WIN = 384
TIME_PIECES = 4
OUT_PIECES = 4
TURNED_PIECES = 2
F32 = jnp.float32
BF16 = jnp.bfloat16
NT_DIMS = (((1,), (1,)), ((), ()))


def time_basis(freq_count, per):
    arg = 2.0 * math.pi * (np.arange(freq_count)[:, None] + 1.0) * np.arange(NTIME)[None, :] / NTIME
    base = 0.5 * np.stack([np.cos(arg), -np.sin(arg)], 1)
    rows = np.repeat(base.reshape(freq_count * 2, NTIME), per, 0).astype(np.float32)
    high = rows.astype(jnp.bfloat16)
    low = (rows - high.astype(np.float32)).astype(jnp.bfloat16)
    return np.concatenate([high, low], 1)


def start_all(*copies):
    for copy in copies:
        copy.start()
    return copies


def coef_kernel(ranks, codes, scale, model, out, plain, rotated, first, pool, ready, out_sems):
    part = pl.program_id(0)
    _, rows, cap = codes.shape
    tiles = ranks.shape[0]
    half = model.shape[1] // 2
    mine = lax.axis_index("tile")
    piece = cap // 2

    @pl.when(part == 0)
    def _():
        for lane in range(2):
            pool[lane, cap:cap + RSLOT + 8, :] = jnp.zeros((RSLOT + 8, 128), F32)
        turned = model[...].astype(F32).T
        plain[...] = turned.astype(BF16)
        rotated[:half] = turned[half:].astype(BF16)
        rotated[half:] = (-turned[:half]).astype(BF16)
        for at in range(0, cap, piece):
            first[:, at:at + piece] = jnp.dot(plain[...], codes[0, :, at:at + piece], preferred_element_type=F32)

    def move(tile, begin):
        for lane in range(2):
            ready[tile, :, lane * 128:lane * 128 + 128] = pool[lane, pl.ds(begin, RSLOT), :].astype(BF16)
        return begin + ranks[tile, mine]

    @pl.when(part == 1)
    def _():
        for at in range(0, cap, piece):
            acc = first[:, at:at + piece] + jnp.dot(rotated[...], codes[0, :, at:at + piece], preferred_element_type=F32)
            upright = (acc * scale[:, at:at + piece]).T
            for lane in range(2):
                pool[lane, at:at + piece, :] = upright[:, lane * 128:lane * 128 + 128]
        begin = jnp.int32(0)
        leaving = []
        per = tiles // OUT_PIECES
        for k in range(OUT_PIECES):
            begin = lax.fori_loop(k * per, k * per + per, move, begin)
            leaving.append(pltpu.make_async_copy(ready.at[pl.ds(k * per, per)], out.at[pl.ds(k * per, per)], out_sems.at[k]))
            leaving[-1].start()
        for copy in leaving:
            copy.wait()


def in_hbm(*arrays):
    return [pltpu.with_memory_space_constraint(array, pltpu.HBM) for array in arrays]


def coef(ranks, codes, scale, model):
    parts, rows, cap = codes.shape
    width = model.shape[1]
    tiles = ranks.shape[0]
    return pl.pallas_call(
        coef_kernel,
        grid=(parts,),
        in_specs=[
            pl.BlockSpec(memory_space=pltpu.SMEM),
            pl.BlockSpec((1, rows, cap), lambda i: (i, 0, 0)),
            pl.BlockSpec(scale.shape, lambda i: (0, 0)),
            pl.BlockSpec(model.shape, lambda i: (0, 0)),
        ],
        out_specs=pl.BlockSpec(memory_space=pl.ANY),
        out_shape=jax.ShapeDtypeStruct((tiles, RSLOT, width), BF16),
        scratch_shapes=[
            pltpu.VMEM((width, rows), BF16),
            pltpu.VMEM((width, rows), BF16),
            pltpu.VMEM((width, cap), F32),
            pltpu.VMEM((2, cap + RSLOT + 8, 128), F32),
            pltpu.VMEM((tiles, RSLOT, width), BF16),
            pltpu.SemaphoreType.DMA((OUT_PIECES,)),
        ],
        compiler_params=pltpu.CompilerParams(vmem_limit_bytes=32 << 20),
        cost_estimate=pl.CostEstimate(flops=4 * cap * rows * width, bytes_accessed=parts * rows * cap * 2, transcendentals=0),
        name="coef",
    )(*in_hbm(ranks, codes, scale, model))


def slot_kernel(by_row, with_turned, ranks, codes, scale, *rest):
    out = rest[0]
    turned = rest[1] if with_turned else None
    begin, rank = rest[-2:]
    step = pl.program_id(0)
    tiles = ranks.shape[0]
    cap = codes.shape[2]
    mine = lax.axis_index("tile")

    @pl.when(step == 0)
    def _():
        def fill(tile, acc):
            here = ranks[mine, tile] if by_row else ranks[tile, mine]
            begin[tile] = acc
            rank[tile] = here
            return acc + here

        lax.fori_loop(0, tiles, fill, jnp.int32(0))

    first_tile = (step * BLK) // RSLOT
    inside = step * BLK - first_tile * RSLOT
    first = begin[first_tile] + jnp.minimum(inside, rank[first_tile])
    start = pl.multiple_of(jnp.minimum((first // 128) * 128, cap - WIN), 128)
    lane = lax.broadcasted_iota(jnp.int32, (1, BLK), 1)
    where_from = jnp.full((1, BLK), -1, jnp.int32)
    for ahead in range(-(-BLK // RSLOT) + 1):
        tile = jnp.minimum(first_tile + ahead, tiles - 1)
        offset = lane + (step * BLK - tile * RSLOT)
        live = (offset >= 0) & (offset < rank[tile])
        where_from = jnp.where(live, offset + (begin[tile] - start), where_from)
    picks = jnp.where(lax.broadcasted_iota(jnp.int32, (WIN, BLK), 0) == where_from, 1.0, 0.0).astype(BF16)
    window = scale[:, pl.ds(start, WIN)]
    high = window.astype(BF16).astype(F32)
    middle = (window - high).astype(BF16).astype(F32)
    low = window - high - middle
    row = lax.broadcasted_iota(jnp.int32, (16, WIN), 0)
    split = jnp.where(row == 0, high, jnp.where(row == 1, middle, jnp.where(row == 2, low, 0.0))).astype(BF16)
    weight = jnp.sum(jnp.dot(split, picks, preferred_element_type=F32), 0, keepdims=True)
    rows = codes.shape[1]
    for part in range(2):
        moved = jnp.dot(codes[part, :, pl.ds(start, WIN)], picks, preferred_element_type=F32) * weight
        out[part] = moved.astype(BF16)
        if with_turned:
            turned[:, part * rows:part * rows + rows] = moved.T.astype(BF16)


def slots(by_row, with_turned, ranks, codes, scale):
    parts, rows, cap = codes.shape
    tiles = ranks.shape[0]
    out_specs = [pl.BlockSpec((parts, rows, BLK), lambda i: (0, 0, i))]
    out_shape = [jax.ShapeDtypeStruct((parts, rows, tiles * RSLOT), BF16)]
    if with_turned:
        out_specs.append(pl.BlockSpec((BLK, parts * rows), lambda i: (i, 0)))
        out_shape.append(jax.ShapeDtypeStruct((tiles * RSLOT, parts * rows), BF16))
    return pl.pallas_call(
        functools.partial(slot_kernel, by_row, with_turned),
        grid=(tiles * RSLOT // BLK,),
        in_specs=[
            pl.BlockSpec(memory_space=pltpu.SMEM),
            pl.BlockSpec((parts, rows, cap), lambda i: (0, 0, 0), pipeline_mode=pl.Buffered(1)),
            pl.BlockSpec((1, cap), lambda i: (0, 0)),
        ],
        out_specs=out_specs,
        out_shape=out_shape,
        scratch_shapes=[pltpu.SMEM((tiles,), jnp.int32), pltpu.SMEM((tiles,), jnp.int32)],
        compiler_params=pltpu.CompilerParams(vmem_limit_bytes=16 << 20),
        cost_estimate=pl.CostEstimate(flops=4 * cap * rows * WIN, bytes_accessed=2 * parts * rows * cap * 2, transcendentals=0),
        name="slot_rows" if by_row else "slot_cols",
    )(ranks, codes, scale)


def complex_rows(stacked, rows, lanes):
    half = lanes // 2
    imag = stacked[rows:]
    swapped = jnp.concatenate([imag[:, half:], imag[:, :half]], 1)
    sign = jnp.where(lax.broadcasted_iota(jnp.int32, (1, lanes), 1) < half, -1.0, 1.0)
    return stacked[:rows] + swapped * sign


def residual_kernel(coefs, factor, turned, data, out, held, real, both, ready, sems, out_sems):
    part = pl.program_id(0)
    _, rows, cap = factor.shape
    lanes = coefs.shape[1]
    half = lanes // 2
    step = cap // TURNED_PIECES
    copies = []
    for k in range(TURNED_PIECES):
        at = pl.ds(k * step, step)
        copies.append(pltpu.make_async_copy(turned.at[at], held.at[at], sems.at[k]))

    @pl.when(part == 0)
    def _():
        for copy in copies:
            copy.start()
        real[...] = jnp.dot(factor[0], coefs[...], preferred_element_type=F32)

    @pl.when(part == 1)
    def _():
        imag = jnp.dot(factor[0], coefs[...], preferred_element_type=F32)
        side = lax.broadcasted_iota(jnp.int32, (1, lanes), 1) < half
        swapped = jnp.concatenate([imag[:, half:], imag[:, :half]], 1)
        rest = (real[...] + swapped * jnp.where(side, -1.0, 1.0) - data[...].astype(F32)).astype(BF16).astype(F32)
        swapped = jnp.concatenate([rest[:, half:], rest[:, :half]], 1)
        both[:rows] = rest.astype(BF16)
        both[rows:] = (swapped * jnp.where(side, 1.0, -1.0)).astype(BF16)
        leaving = []
        weights = both[...]
        for k in range(TURNED_PIECES):
            copies[k].wait()
            at = slice(k * step, k * step + step)
            ready[at] = jnp.dot(held[at], weights, preferred_element_type=F32).astype(BF16)
            leaving.append(pltpu.make_async_copy(ready.at[at], out.at[at], out_sems.at[k]))
            leaving[-1].start()
        for copy in leaving:
            copy.wait()


def residual(coefs, factor, turned, data):
    parts, rows, cap = factor.shape
    lanes = coefs.shape[1]
    hbm = pl.BlockSpec(memory_space=pl.ANY)
    return pl.pallas_call(
        residual_kernel,
        grid=(parts,),
        in_specs=[
            pl.BlockSpec((cap, lanes), lambda i: (0, 0)),
            pl.BlockSpec((1, rows, cap), lambda i: (i, 0, 0)),
            hbm,
            pl.BlockSpec((rows, lanes), lambda i: (0, 0)),
        ],
        out_specs=hbm,
        out_shape=jax.ShapeDtypeStruct((cap, lanes), BF16),
        scratch_shapes=[
            pltpu.VMEM((cap, parts * rows), BF16),
            pltpu.VMEM((rows, lanes), F32),
            pltpu.VMEM((parts * rows, lanes), BF16),
            pltpu.VMEM((cap, lanes), BF16),
            pltpu.SemaphoreType.DMA((TURNED_PIECES,)),
            pltpu.SemaphoreType.DMA((TURNED_PIECES,)),
        ],
        compiler_params=pltpu.CompilerParams(vmem_limit_bytes=32 << 20),
        cost_estimate=pl.CostEstimate(flops=8 * cap * rows * lanes, bytes_accessed=2 * cap * lanes * 2, transcendentals=0),
        name="residual",
    )(coefs, *in_hbm(factor, turned), data)


def gradient_kernel(coefs, factor, out, real):
    part = pl.program_id(0)
    _, rows, cap = factor.shape
    lanes = coefs.shape[1]

    @pl.when(part == 0)
    def _():
        real[...] = jnp.dot(factor[0], coefs[...], preferred_element_type=F32)

    @pl.when(part == 1)
    def _():
        imag = jnp.dot(factor[0], coefs[...], preferred_element_type=F32)
        half_lanes = lanes // 2
        swapped = jnp.concatenate([imag[:, half_lanes:], imag[:, :half_lanes]], 1)
        sign = jnp.where(lax.broadcasted_iota(jnp.int32, (1, lanes), 1) < half_lanes, -1.0, 1.0)
        flipped = (real[...] + swapped * sign).T
        owners, each, _ = out.shape
        half = each // 2
        for owner in range(owners):
            for ri in range(2):
                at = ri * (lanes // 2) + owner * half
                out[owner, ri * half:ri * half + half, :] = flipped[at:at + half].astype(BF16)


def gradient(coefs, factor, owners):
    parts, rows, cap = factor.shape
    lanes = coefs.shape[1]
    return pl.pallas_call(
        gradient_kernel,
        grid=(parts,),
        in_specs=[pl.BlockSpec((cap, lanes), lambda i: (0, 0)), pl.BlockSpec((1, rows, cap), lambda i: (i, 0, 0))],
        out_specs=pl.BlockSpec((owners, lanes // owners, rows), lambda i: (0, 0, 0)),
        out_shape=jax.ShapeDtypeStruct((owners, lanes // owners, rows), BF16),
        scratch_shapes=[pltpu.VMEM((rows, lanes), F32)],
        compiler_params=pltpu.CompilerParams(vmem_limit_bytes=20 << 20),
        cost_estimate=pl.CostEstimate(flops=4 * cap * rows * lanes, bytes_accessed=cap * lanes * 2, transcendentals=0),
        name="gradient",
    )(coefs, *in_hbm(factor))


def time_kernel(mute, arrived, basis, out, spectra, ready, sems):
    rows, share, times = ready.shape
    depth = basis.shape[0]
    here = rows // sems.shape[0]
    spectra[...] = arrived[...].reshape(depth, rows).astype(F32).T
    lane = lax.broadcasted_iota(jnp.int32, (share, depth), 1)
    row = lax.broadcasted_iota(jnp.int32, (share, depth), 0)
    own = row == lane % share
    when = lax.broadcasted_iota(jnp.int32, (share, times), 1)

    def leaving(step):
        at = pl.ds(step * here, here)
        return pltpu.make_async_copy(ready.at[at], out.at[at], sems.at[step])

    def push(step, carry):
        base = step * here
        lines = []
        for n in range(here):
            lines.append(jnp.where(own, spectra[pl.ds(base + n, 1), :], 0.0).astype(BF16))
        got = jnp.dot(jnp.concatenate(lines, 0), basis[...], preferred_element_type=F32)
        signal = got[:, :times] + got[:, times:]
        for n in range(here):
            ready[base + n] = jnp.where(when >= mute[base + n], signal[n * share:n * share + share], 0.0).astype(BF16)
        leaving(step).start()
        return carry

    def finish(step, carry):
        leaving(step).wait()
        return carry

    lax.fori_loop(0, sems.shape[0], push, 0)
    lax.fori_loop(0, sems.shape[0], finish, 0)


def to_time(mute, arrived, basis, rows, share):
    vmem = pl.BlockSpec(memory_space=pltpu.VMEM)
    return pl.pallas_call(
        time_kernel,
        in_specs=[pl.BlockSpec(memory_space=pltpu.SMEM), vmem, vmem],
        out_specs=pl.BlockSpec(memory_space=pl.ANY),
        out_shape=jax.ShapeDtypeStruct((rows, share, NTIME), BF16),
        scratch_shapes=[
            pltpu.VMEM((rows, basis.shape[0]), F32),
            pltpu.VMEM((rows, share, NTIME), BF16),
            pltpu.SemaphoreType.DMA((TIME_PIECES,)),
        ],
        compiler_params=pltpu.CompilerParams(vmem_limit_bytes=16 << 20),
        name="to_time",
    )(mute, arrived, basis)


def shards(model_field, data_field, u_codes, u_scales, v_codes, v_scales, tile_ranks, mute_start):
    ranks = tile_ranks[0]
    tiles = ranks.shape[0]
    rows = model_field.shape[1]
    width = model_field.shape[2]
    freq_count = lax.axis_size("freq")
    sources = width // 2
    share = sources // freq_count
    basis = jnp.asarray(time_basis(freq_count, share))
    sent = coef(ranks, v_codes[0], v_scales[0], model_field[0])
    late_u, late_v, sent = lax.optimization_barrier((u_codes[0], v_codes[0], sent))
    arrived = lax.all_to_all(sent, "tile", split_axis=0, concat_axis=0, tiled=True)
    u_slots, u_turned = slots(True, True, ranks, late_u, u_scales[0])
    v_slots, = slots(False, False, ranks, late_v, v_scales[0])
    back = residual(arrived.reshape(tiles * RSLOT, width), u_slots, u_turned, data_field[0])
    back = lax.all_to_all(back.reshape(tiles, RSLOT, width), "tile", split_axis=0, concat_axis=0, tiled=True)
    part = gradient(back.reshape(tiles * RSLOT, width), v_slots, freq_count)
    spectra = lax.all_to_all(part, "freq", split_axis=0, concat_axis=0, tiled=True)
    return to_time(mute_start, spectra, basis, rows, share)


def solution(mesh):
    in_specs = (
        P("freq", "tile", None),
        P("freq", "tile", None),
        P("freq", None, "tile", None),
        P("freq", "tile", None),
        P("freq", None, "tile", None),
        P("freq", "tile", None),
        P("freq", None, None),
        P("tile"),
    )
    out_specs = P("tile", "freq", None)
    return jax.shard_map(shards, mesh=mesh, in_specs=in_specs, out_specs=out_specs, check_vma=False)
```

```python
import functools
import math

import jax
import jax.numpy as jnp
import numpy as np
from jax import lax
from jax.experimental import pallas as pl
from jax.experimental.pallas import tpu as pltpu
from jax.sharding import PartitionSpec as P

RSLOT = 88
NTIME = 128
BLK = 256
WIN = 384
STAGGER_NS = 18000
TIME_PIECES = 4
OUT_PIECES = 4
TURNED_PIECES = 2
F32 = jnp.float32
BF16 = jnp.bfloat16
NT_DIMS = (((1,), (1,)), ((), ()))


def time_basis(freq_count, per):
    arg = 2.0 * math.pi * (np.arange(freq_count)[:, None] + 1.0) * np.arange(NTIME)[None, :] / NTIME
    base = 0.5 * np.stack([np.cos(arg), -np.sin(arg)], 1)
    rows = np.repeat(base.reshape(freq_count * 2, NTIME), per, 0).astype(np.float32)
    high = rows.astype(jnp.bfloat16)
    low = (rows - high.astype(np.float32)).astype(jnp.bfloat16)
    return np.concatenate([high, low], 1)


def start_all(*copies):
    for copy in copies:
        copy.start()
    return copies


def coef_kernel(ranks, codes, scale, model, out, plain, rotated, first, pool, ready, out_sems):
    part = pl.program_id(0)
    _, rows, cap = codes.shape
    tiles = ranks.shape[0]
    half = model.shape[1] // 2
    mine = lax.axis_index("tile")
    piece = cap // 2

    @pl.when(part == 0)
    def _():
        for lane in range(2):
            pool[lane, cap:cap + RSLOT + 8, :] = jnp.zeros((RSLOT + 8, 128), F32)
        turned = model[...].astype(F32).T
        plain[...] = turned.astype(BF16)
        rotated[:half] = turned[half:].astype(BF16)
        rotated[half:] = (-turned[:half]).astype(BF16)
        for at in range(0, cap, piece):
            first[:, at:at + piece] = jnp.dot(plain[...], codes[0, :, at:at + piece], preferred_element_type=F32)

    def move(tile, begin):
        for lane in range(2):
            ready[tile, :, lane * 128:lane * 128 + 128] = pool[lane, pl.ds(begin, RSLOT), :].astype(BF16)
        return begin + ranks[tile, mine]

    @pl.when(part == 1)
    def _():
        for at in range(0, cap, piece):
            acc = first[:, at:at + piece] + jnp.dot(rotated[...], codes[0, :, at:at + piece], preferred_element_type=F32)
            upright = (acc * scale[:, at:at + piece]).T
            for lane in range(2):
                pool[lane, at:at + piece, :] = upright[:, lane * 128:lane * 128 + 128]
        begin = jnp.int32(0)
        leaving = []
        per = tiles // OUT_PIECES
        for k in range(OUT_PIECES):
            begin = lax.fori_loop(k * per, k * per + per, move, begin)
            leaving.append(pltpu.make_async_copy(ready.at[pl.ds(k * per, per)], out.at[pl.ds(k * per, per)], out_sems.at[k]))
            leaving[-1].start()
        for copy in leaving:
            copy.wait()

        @pl.when(lax.axis_index("freq") % 2 == 1)
        def _():
            pl.delay(STAGGER_NS)


def in_hbm(*arrays):
    return [pltpu.with_memory_space_constraint(array, pltpu.HBM) for array in arrays]


def coef(ranks, codes, scale, model):
    parts, rows, cap = codes.shape
    width = model.shape[1]
    tiles = ranks.shape[0]
    return pl.pallas_call(
        coef_kernel,
        grid=(parts,),
        in_specs=[
            pl.BlockSpec(memory_space=pltpu.SMEM),
            pl.BlockSpec((1, rows, cap), lambda i: (i, 0, 0)),
            pl.BlockSpec(scale.shape, lambda i: (0, 0)),
            pl.BlockSpec(model.shape, lambda i: (0, 0)),
        ],
        out_specs=pl.BlockSpec(memory_space=pl.ANY),
        out_shape=jax.ShapeDtypeStruct((tiles, RSLOT, width), BF16),
        scratch_shapes=[
            pltpu.VMEM((width, rows), BF16),
            pltpu.VMEM((width, rows), BF16),
            pltpu.VMEM((width, cap), F32),
            pltpu.VMEM((2, cap + RSLOT + 8, 128), F32),
            pltpu.VMEM((tiles, RSLOT, width), BF16),
            pltpu.SemaphoreType.DMA((OUT_PIECES,)),
        ],
        compiler_params=pltpu.CompilerParams(vmem_limit_bytes=32 << 20),
        cost_estimate=pl.CostEstimate(flops=4 * cap * rows * width, bytes_accessed=parts * rows * cap * 2, transcendentals=0),
        name="coef",
    )(*in_hbm(ranks, codes, scale, model))


def slot_kernel(by_row, with_turned, ranks, codes, scale, *rest):
    out = rest[0]
    turned = rest[1] if with_turned else None
    begin, rank = rest[-2:]
    step = pl.program_id(0)
    tiles = ranks.shape[0]
    cap = codes.shape[2]
    mine = lax.axis_index("tile")

    @pl.when(step == 0)
    def _():
        def fill(tile, acc):
            here = ranks[mine, tile] if by_row else ranks[tile, mine]
            begin[tile] = acc
            rank[tile] = here
            return acc + here

        lax.fori_loop(0, tiles, fill, jnp.int32(0))

    first_tile = (step * BLK) // RSLOT
    inside = step * BLK - first_tile * RSLOT
    first = begin[first_tile] + jnp.minimum(inside, rank[first_tile])
    start = pl.multiple_of(jnp.minimum((first // 128) * 128, cap - WIN), 128)
    lane = lax.broadcasted_iota(jnp.int32, (1, BLK), 1)
    where_from = jnp.full((1, BLK), -1, jnp.int32)
    for ahead in range(-(-BLK // RSLOT) + 1):
        tile = jnp.minimum(first_tile + ahead, tiles - 1)
        offset = lane + (step * BLK - tile * RSLOT)
        live = (offset >= 0) & (offset < rank[tile])
        where_from = jnp.where(live, offset + (begin[tile] - start), where_from)
    picks = jnp.where(lax.broadcasted_iota(jnp.int32, (WIN, BLK), 0) == where_from, 1.0, 0.0).astype(BF16)
    window = scale[:, pl.ds(start, WIN)]
    high = window.astype(BF16).astype(F32)
    middle = (window - high).astype(BF16).astype(F32)
    low = window - high - middle
    row = lax.broadcasted_iota(jnp.int32, (16, WIN), 0)
    split = jnp.where(row == 0, high, jnp.where(row == 1, middle, jnp.where(row == 2, low, 0.0))).astype(BF16)
    weight = jnp.sum(jnp.dot(split, picks, preferred_element_type=F32), 0, keepdims=True)
    rows = codes.shape[1]
    for part in range(2):
        moved = jnp.dot(codes[part, :, pl.ds(start, WIN)], picks, preferred_element_type=F32) * weight
        out[part] = moved.astype(BF16)
        if with_turned:
            turned[:, part * rows:part * rows + rows] = moved.T.astype(BF16)


def slots(by_row, with_turned, ranks, codes, scale):
    parts, rows, cap = codes.shape
    tiles = ranks.shape[0]
    out_specs = [pl.BlockSpec((parts, rows, BLK), lambda i: (0, 0, i))]
    out_shape = [jax.ShapeDtypeStruct((parts, rows, tiles * RSLOT), BF16)]
    if with_turned:
        out_specs.append(pl.BlockSpec((BLK, parts * rows), lambda i: (i, 0)))
        out_shape.append(jax.ShapeDtypeStruct((tiles * RSLOT, parts * rows), BF16))
    return pl.pallas_call(
        functools.partial(slot_kernel, by_row, with_turned),
        grid=(tiles * RSLOT // BLK,),
        in_specs=[
            pl.BlockSpec(memory_space=pltpu.SMEM),
            pl.BlockSpec((parts, rows, cap), lambda i: (0, 0, 0), pipeline_mode=pl.Buffered(1)),
            pl.BlockSpec((1, cap), lambda i: (0, 0)),
        ],
        out_specs=out_specs,
        out_shape=out_shape,
        scratch_shapes=[pltpu.SMEM((tiles,), jnp.int32), pltpu.SMEM((tiles,), jnp.int32)],
        compiler_params=pltpu.CompilerParams(vmem_limit_bytes=16 << 20),
        cost_estimate=pl.CostEstimate(flops=4 * cap * rows * WIN, bytes_accessed=2 * parts * rows * cap * 2, transcendentals=0),
        name="slot_rows" if by_row else "slot_cols",
    )(ranks, codes, scale)


def complex_rows(stacked, rows, lanes):
    half = lanes // 2
    imag = stacked[rows:]
    swapped = jnp.concatenate([imag[:, half:], imag[:, :half]], 1)
    sign = jnp.where(lax.broadcasted_iota(jnp.int32, (1, lanes), 1) < half, -1.0, 1.0)
    return stacked[:rows] + swapped * sign


def residual_kernel(coefs, factor, turned, data, out, held, real, both, ready, sems, out_sems):
    part = pl.program_id(0)
    _, rows, cap = factor.shape
    lanes = coefs.shape[1]
    half = lanes // 2
    step = cap // TURNED_PIECES
    copies = []
    for k in range(TURNED_PIECES):
        at = pl.ds(k * step, step)
        copies.append(pltpu.make_async_copy(turned.at[at], held.at[at], sems.at[k]))

    @pl.when(part == 0)
    def _():
        for copy in copies:
            copy.start()
        real[...] = jnp.dot(factor[0], coefs[...], preferred_element_type=F32)

    @pl.when(part == 1)
    def _():
        imag = jnp.dot(factor[0], coefs[...], preferred_element_type=F32)
        side = lax.broadcasted_iota(jnp.int32, (1, lanes), 1) < half
        swapped = jnp.concatenate([imag[:, half:], imag[:, :half]], 1)
        rest = (real[...] + swapped * jnp.where(side, -1.0, 1.0) - data[...].astype(F32)).astype(BF16).astype(F32)
        swapped = jnp.concatenate([rest[:, half:], rest[:, :half]], 1)
        both[:rows] = rest.astype(BF16)
        both[rows:] = (swapped * jnp.where(side, 1.0, -1.0)).astype(BF16)
        leaving = []
        weights = both[...]
        for k in range(TURNED_PIECES):
            copies[k].wait()
            at = slice(k * step, k * step + step)
            ready[at] = jnp.dot(held[at], weights, preferred_element_type=F32).astype(BF16)
            leaving.append(pltpu.make_async_copy(ready.at[at], out.at[at], out_sems.at[k]))
            leaving[-1].start()
        for copy in leaving:
            copy.wait()


def residual(coefs, factor, turned, data):
    parts, rows, cap = factor.shape
    lanes = coefs.shape[1]
    hbm = pl.BlockSpec(memory_space=pl.ANY)
    return pl.pallas_call(
        residual_kernel,
        grid=(parts,),
        in_specs=[
            pl.BlockSpec((cap, lanes), lambda i: (0, 0)),
            pl.BlockSpec((1, rows, cap), lambda i: (i, 0, 0)),
            hbm,
            pl.BlockSpec((rows, lanes), lambda i: (0, 0)),
        ],
        out_specs=hbm,
        out_shape=jax.ShapeDtypeStruct((cap, lanes), BF16),
        scratch_shapes=[
            pltpu.VMEM((cap, parts * rows), BF16),
            pltpu.VMEM((rows, lanes), F32),
            pltpu.VMEM((parts * rows, lanes), BF16),
            pltpu.VMEM((cap, lanes), BF16),
            pltpu.SemaphoreType.DMA((TURNED_PIECES,)),
            pltpu.SemaphoreType.DMA((TURNED_PIECES,)),
        ],
        compiler_params=pltpu.CompilerParams(vmem_limit_bytes=32 << 20),
        cost_estimate=pl.CostEstimate(flops=8 * cap * rows * lanes, bytes_accessed=2 * cap * lanes * 2, transcendentals=0),
        name="residual",
    )(coefs, *in_hbm(factor, turned), data)


def gradient_kernel(coefs, factor, out, real):
    part = pl.program_id(0)
    _, rows, cap = factor.shape
    lanes = coefs.shape[1]

    @pl.when(part == 0)
    def _():
        real[...] = jnp.dot(factor[0], coefs[...], preferred_element_type=F32)

    @pl.when(part == 1)
    def _():
        imag = jnp.dot(factor[0], coefs[...], preferred_element_type=F32)
        half_lanes = lanes // 2
        swapped = jnp.concatenate([imag[:, half_lanes:], imag[:, :half_lanes]], 1)
        sign = jnp.where(lax.broadcasted_iota(jnp.int32, (1, lanes), 1) < half_lanes, -1.0, 1.0)
        flipped = (real[...] + swapped * sign).T
        owners, each, _ = out.shape
        half = each // 2
        for owner in range(owners):
            for ri in range(2):
                at = ri * (lanes // 2) + owner * half
                out[owner, ri * half:ri * half + half, :] = flipped[at:at + half].astype(BF16)


def gradient(coefs, factor, owners):
    parts, rows, cap = factor.shape
    lanes = coefs.shape[1]
    return pl.pallas_call(
        gradient_kernel,
        grid=(parts,),
        in_specs=[pl.BlockSpec((cap, lanes), lambda i: (0, 0)), pl.BlockSpec((1, rows, cap), lambda i: (i, 0, 0))],
        out_specs=pl.BlockSpec((owners, lanes // owners, rows), lambda i: (0, 0, 0)),
        out_shape=jax.ShapeDtypeStruct((owners, lanes // owners, rows), BF16),
        scratch_shapes=[pltpu.VMEM((rows, lanes), F32)],
        compiler_params=pltpu.CompilerParams(vmem_limit_bytes=20 << 20),
        cost_estimate=pl.CostEstimate(flops=4 * cap * rows * lanes, bytes_accessed=cap * lanes * 2, transcendentals=0),
        name="gradient",
    )(coefs, *in_hbm(factor))


def time_kernel(mute, arrived, basis, out, spectra, ready, sems):
    rows, share, times = ready.shape
    depth = basis.shape[0]
    here = rows // sems.shape[0]
    spectra[...] = arrived[...].reshape(depth, rows).astype(F32).T
    lane = lax.broadcasted_iota(jnp.int32, (share, depth), 1)
    row = lax.broadcasted_iota(jnp.int32, (share, depth), 0)
    own = row == lane % share
    when = lax.broadcasted_iota(jnp.int32, (share, times), 1)

    def leaving(step):
        at = pl.ds(step * here, here)
        return pltpu.make_async_copy(ready.at[at], out.at[at], sems.at[step])

    def push(step, carry):
        base = step * here
        lines = []
        for n in range(here):
            lines.append(jnp.where(own, spectra[pl.ds(base + n, 1), :], 0.0).astype(BF16))
        got = jnp.dot(jnp.concatenate(lines, 0), basis[...], preferred_element_type=F32)
        signal = got[:, :times] + got[:, times:]
        for n in range(here):
            ready[base + n] = jnp.where(when >= mute[base + n], signal[n * share:n * share + share], 0.0).astype(BF16)
        leaving(step).start()
        return carry

    def finish(step, carry):
        leaving(step).wait()
        return carry

    lax.fori_loop(0, sems.shape[0], push, 0)
    lax.fori_loop(0, sems.shape[0], finish, 0)


def to_time(mute, arrived, basis, rows, share):
    vmem = pl.BlockSpec(memory_space=pltpu.VMEM)
    return pl.pallas_call(
        time_kernel,
        in_specs=[pl.BlockSpec(memory_space=pltpu.SMEM), vmem, vmem],
        out_specs=pl.BlockSpec(memory_space=pl.ANY),
        out_shape=jax.ShapeDtypeStruct((rows, share, NTIME), BF16),
        scratch_shapes=[
            pltpu.VMEM((rows, basis.shape[0]), F32),
            pltpu.VMEM((rows, share, NTIME), BF16),
            pltpu.SemaphoreType.DMA((TIME_PIECES,)),
        ],
        compiler_params=pltpu.CompilerParams(vmem_limit_bytes=16 << 20),
        name="to_time",
    )(mute, arrived, basis)


def shards(model_field, data_field, u_codes, u_scales, v_codes, v_scales, tile_ranks, mute_start):
    ranks = tile_ranks[0]
    tiles = ranks.shape[0]
    rows = model_field.shape[1]
    width = model_field.shape[2]
    freq_count = lax.axis_size("freq")
    sources = width // 2
    share = sources // freq_count
    basis = jnp.asarray(time_basis(freq_count, share))
    sent = coef(ranks, v_codes[0], v_scales[0], model_field[0])
    late_u, late_v, sent = lax.optimization_barrier((u_codes[0], v_codes[0], sent))
    arrived = lax.all_to_all(sent, "tile", split_axis=0, concat_axis=0, tiled=True)
    u_slots, u_turned = slots(True, True, ranks, late_u, u_scales[0])
    v_slots, = slots(False, False, ranks, late_v, v_scales[0])
    back = residual(arrived.reshape(tiles * RSLOT, width), u_slots, u_turned, data_field[0])
    back = lax.all_to_all(back.reshape(tiles, RSLOT, width), "tile", split_axis=0, concat_axis=0, tiled=True)
    part = gradient(back.reshape(tiles * RSLOT, width), v_slots, freq_count)
    spectra = lax.all_to_all(part, "freq", split_axis=0, concat_axis=0, tiled=True)
    return to_time(mute_start, spectra, basis, rows, share)


def solution(mesh):
    in_specs = (
        P("freq", "tile", None),
        P("freq", "tile", None),
        P("freq", None, "tile", None),
        P("freq", "tile", None),
        P("freq", None, "tile", None),
        P("freq", "tile", None),
        P("freq", None, None),
        P("tile"),
    )
    out_specs = P("tile", "freq", None)
    return jax.shard_map(shards, mesh=mesh, in_specs=in_specs, out_specs=out_specs, check_vma=False)
```

```python
import functools
import math

import jax
import jax.numpy as jnp
import numpy as np
from jax import lax
from jax.experimental import pallas as pl
from jax.experimental.pallas import tpu as pltpu
from jax.sharding import PartitionSpec as P

RSLOT = 88
NTIME = 128
BLK = 256
WIN = 384
STAGGER_NS = 18000
TIME_PIECES = 8
OUT_PIECES = 4
TURNED_SIXTEENTHS = (8,)
F32 = jnp.float32
BF16 = jnp.bfloat16
NT_DIMS = (((1,), (1,)), ((), ()))


def time_basis(freq_count, per):
    arg = 2.0 * math.pi * (np.arange(freq_count)[:, None] + 1.0) * np.arange(NTIME)[None, :] / NTIME
    base = 0.5 * np.stack([np.cos(arg), -np.sin(arg)], 1)
    rows = np.repeat(base.reshape(freq_count * 2, NTIME), per, 0).astype(np.float32)
    high = rows.astype(jnp.bfloat16)
    low = (rows - high.astype(np.float32)).astype(jnp.bfloat16)
    return np.concatenate([high, low], 1)


def start_all(*copies):
    for copy in copies:
        copy.start()
    return copies


def coef_kernel(ranks, codes, scale, model, out, plain, rotated, first, pool, ready, out_sems):
    part = pl.program_id(0)
    _, rows, cap = codes.shape
    tiles = ranks.shape[0]
    half = model.shape[1] // 2
    mine = lax.axis_index("tile")
    piece = cap // 2

    @pl.when(part == 0)
    def _():
        for lane in range(2):
            pool[lane, cap:cap + RSLOT + 8, :] = jnp.zeros((RSLOT + 8, 128), F32)
        turned = model[...].astype(F32).T
        plain[...] = turned.astype(BF16)
        rotated[:half] = turned[half:].astype(BF16)
        rotated[half:] = (-turned[:half]).astype(BF16)
        for at in range(0, cap, piece):
            first[:, at:at + piece] = jnp.dot(plain[...], codes[0, :, at:at + piece], preferred_element_type=F32)

    def move(tile, begin):
        for lane in range(2):
            ready[tile, :, lane * 128:lane * 128 + 128] = pool[lane, pl.ds(begin, RSLOT), :].astype(BF16)
        return begin + ranks[tile, mine]

    @pl.when(part == 1)
    def _():
        for at in range(0, cap, piece):
            acc = first[:, at:at + piece] + jnp.dot(rotated[...], codes[0, :, at:at + piece], preferred_element_type=F32)
            upright = (acc * scale[:, at:at + piece]).T
            for lane in range(2):
                pool[lane, at:at + piece, :] = upright[:, lane * 128:lane * 128 + 128]
        begin = jnp.int32(0)
        leaving = []
        per = tiles // OUT_PIECES
        for k in range(OUT_PIECES):
            begin = lax.fori_loop(k * per, k * per + per, move, begin)
            leaving.append(pltpu.make_async_copy(ready.at[pl.ds(k * per, per)], out.at[pl.ds(k * per, per)], out_sems.at[k]))
            leaving[-1].start()
        for copy in leaving:
            copy.wait()

        @pl.when(lax.axis_index("freq") % 2 == 1)
        def _():
            pl.delay(STAGGER_NS)


def in_hbm(*arrays):
    return [pltpu.with_memory_space_constraint(array, pltpu.HBM) for array in arrays]


def coef(ranks, codes, scale, model):
    parts, rows, cap = codes.shape
    width = model.shape[1]
    tiles = ranks.shape[0]
    return pl.pallas_call(
        coef_kernel,
        grid=(parts,),
        in_specs=[
            pl.BlockSpec(memory_space=pltpu.SMEM),
            pl.BlockSpec((1, rows, cap), lambda i: (i, 0, 0)),
            pl.BlockSpec(scale.shape, lambda i: (0, 0)),
            pl.BlockSpec(model.shape, lambda i: (0, 0)),
        ],
        out_specs=pl.BlockSpec(memory_space=pl.ANY),
        out_shape=jax.ShapeDtypeStruct((tiles, RSLOT, width), BF16),
        scratch_shapes=[
            pltpu.VMEM((width, rows), BF16),
            pltpu.VMEM((width, rows), BF16),
            pltpu.VMEM((width, cap), F32),
            pltpu.VMEM((2, cap + RSLOT + 8, 128), F32),
            pltpu.VMEM((tiles, RSLOT, width), BF16),
            pltpu.SemaphoreType.DMA((OUT_PIECES,)),
        ],
        compiler_params=pltpu.CompilerParams(vmem_limit_bytes=32 << 20),
        cost_estimate=pl.CostEstimate(flops=4 * cap * rows * width, bytes_accessed=parts * rows * cap * 2, transcendentals=0),
        name="coef",
    )(*in_hbm(ranks, codes, scale, model))


def slot_kernel(by_row, with_turned, ranks, codes, scale, *rest):
    out = rest[0]
    turned = rest[1] if with_turned else None
    begin, rank = rest[-2:]
    step = pl.program_id(0)
    tiles = ranks.shape[0]
    cap = codes.shape[2]
    mine = lax.axis_index("tile")

    @pl.when(step == 0)
    def _():
        def fill(tile, acc):
            here = ranks[mine, tile] if by_row else ranks[tile, mine]
            begin[tile] = acc
            rank[tile] = here
            return acc + here

        lax.fori_loop(0, tiles, fill, jnp.int32(0))

    first_tile = (step * BLK) // RSLOT
    inside = step * BLK - first_tile * RSLOT
    first = begin[first_tile] + jnp.minimum(inside, rank[first_tile])
    start = pl.multiple_of(jnp.minimum((first // 128) * 128, cap - WIN), 128)
    lane = lax.broadcasted_iota(jnp.int32, (1, BLK), 1)
    where_from = jnp.full((1, BLK), -1, jnp.int32)
    for ahead in range(-(-BLK // RSLOT) + 1):
        tile = jnp.minimum(first_tile + ahead, tiles - 1)
        offset = lane + (step * BLK - tile * RSLOT)
        live = (offset >= 0) & (offset < rank[tile])
        where_from = jnp.where(live, offset + (begin[tile] - start), where_from)
    picks = jnp.where(lax.broadcasted_iota(jnp.int32, (WIN, BLK), 0) == where_from, 1.0, 0.0).astype(BF16)
    window = scale[:, pl.ds(start, WIN)]
    high = window.astype(BF16).astype(F32)
    middle = (window - high).astype(BF16).astype(F32)
    low = window - high - middle
    row = lax.broadcasted_iota(jnp.int32, (16, WIN), 0)
    split = jnp.where(row == 0, high, jnp.where(row == 1, middle, jnp.where(row == 2, low, 0.0))).astype(BF16)
    weight = jnp.sum(jnp.dot(split, picks, preferred_element_type=F32), 0, keepdims=True)
    rows = codes.shape[1]
    for part in range(2):
        moved = jnp.dot(codes[part, :, pl.ds(start, WIN)], picks, preferred_element_type=F32) * weight
        out[part] = moved.astype(BF16)
        if with_turned:
            turned[:, part * rows:part * rows + rows] = moved.T.astype(BF16)


def slots(by_row, with_turned, ranks, codes, scale):
    parts, rows, cap = codes.shape
    tiles = ranks.shape[0]
    out_specs = [pl.BlockSpec((parts, rows, BLK), lambda i: (0, 0, i))]
    out_shape = [jax.ShapeDtypeStruct((parts, rows, tiles * RSLOT), BF16)]
    if with_turned:
        out_specs.append(pl.BlockSpec((BLK, parts * rows), lambda i: (i, 0)))
        out_shape.append(jax.ShapeDtypeStruct((tiles * RSLOT, parts * rows), BF16))
    return pl.pallas_call(
        functools.partial(slot_kernel, by_row, with_turned),
        grid=(tiles * RSLOT // BLK,),
        in_specs=[
            pl.BlockSpec(memory_space=pltpu.SMEM),
            pl.BlockSpec((parts, rows, cap), lambda i: (0, 0, 0), pipeline_mode=pl.Buffered(1)),
            pl.BlockSpec((1, cap), lambda i: (0, 0)),
        ],
        out_specs=out_specs,
        out_shape=out_shape,
        scratch_shapes=[pltpu.SMEM((tiles,), jnp.int32), pltpu.SMEM((tiles,), jnp.int32)],
        compiler_params=pltpu.CompilerParams(vmem_limit_bytes=16 << 20),
        cost_estimate=pl.CostEstimate(flops=4 * cap * rows * WIN, bytes_accessed=2 * parts * rows * cap * 2, transcendentals=0),
        name="slot_rows" if by_row else "slot_cols",
    )(ranks, codes, scale)


def complex_rows(stacked, rows, lanes):
    half = lanes // 2
    imag = stacked[rows:]
    swapped = jnp.concatenate([imag[:, half:], imag[:, :half]], 1)
    sign = jnp.where(lax.broadcasted_iota(jnp.int32, (1, lanes), 1) < half, -1.0, 1.0)
    return stacked[:rows] + swapped * sign


def piece_spans(total):
    spans, first = [], 0
    for part in TURNED_SIXTEENTHS:
        spans.append((first, total // 176 * 11 * part))
        first += spans[-1][1]
    return spans + [(first, total - first)]


def residual_kernel(coefs, factor, turned, data, out, held, real, both, ready, sems, out_sems):
    part = pl.program_id(0)
    _, rows, cap = factor.shape
    lanes = coefs.shape[1]
    half = lanes // 2
    spans = piece_spans(cap)
    copies = []
    for k, (first, size) in enumerate(spans):
        at = pl.ds(first, size)
        copies.append(pltpu.make_async_copy(turned.at[at], held.at[at], sems.at[k]))

    @pl.when(part == 0)
    def _():
        for copy in copies:
            copy.start()
        real[...] = jnp.dot(factor[0], coefs[...], preferred_element_type=F32)

    @pl.when(part == 1)
    def _():
        imag = jnp.dot(factor[0], coefs[...], preferred_element_type=F32)
        side = lax.broadcasted_iota(jnp.int32, (1, lanes), 1) < half
        swapped = jnp.concatenate([imag[:, half:], imag[:, :half]], 1)
        rest = (real[...] + swapped * jnp.where(side, -1.0, 1.0) - data[...].astype(F32)).astype(BF16).astype(F32)
        swapped = jnp.concatenate([rest[:, half:], rest[:, :half]], 1)
        both[:rows] = rest.astype(BF16)
        both[rows:] = (swapped * jnp.where(side, 1.0, -1.0)).astype(BF16)
        leaving = []
        weights = both[...]
        for k, (first, size) in enumerate(spans):
            copies[k].wait()
            at = slice(first, first + size)
            ready[at] = jnp.dot(held[at], weights, preferred_element_type=F32).astype(BF16)
            leaving.append(pltpu.make_async_copy(ready.at[at], out.at[at], out_sems.at[k]))
            leaving[-1].start()
        for copy in leaving:
            copy.wait()


def residual(coefs, factor, turned, data):
    parts, rows, cap = factor.shape
    lanes = coefs.shape[1]
    hbm = pl.BlockSpec(memory_space=pl.ANY)
    return pl.pallas_call(
        residual_kernel,
        grid=(parts,),
        in_specs=[
            pl.BlockSpec((cap, lanes), lambda i: (0, 0)),
            pl.BlockSpec((1, rows, cap), lambda i: (i, 0, 0)),
            hbm,
            pl.BlockSpec((rows, lanes), lambda i: (0, 0)),
        ],
        out_specs=hbm,
        out_shape=jax.ShapeDtypeStruct((cap, lanes), BF16),
        scratch_shapes=[
            pltpu.VMEM((cap, parts * rows), BF16),
            pltpu.VMEM((rows, lanes), F32),
            pltpu.VMEM((parts * rows, lanes), BF16),
            pltpu.VMEM((cap, lanes), BF16),
            pltpu.SemaphoreType.DMA((len(TURNED_SIXTEENTHS) + 1,)),
            pltpu.SemaphoreType.DMA((len(TURNED_SIXTEENTHS) + 1,)),
        ],
        compiler_params=pltpu.CompilerParams(vmem_limit_bytes=32 << 20),
        cost_estimate=pl.CostEstimate(flops=8 * cap * rows * lanes, bytes_accessed=2 * cap * lanes * 2, transcendentals=0),
        name="residual",
    )(coefs, *in_hbm(factor, turned), data)


def gradient_kernel(coefs, factor, out, real):
    part = pl.program_id(0)
    _, rows, cap = factor.shape
    lanes = coefs.shape[1]

    @pl.when(part == 0)
    def _():
        real[...] = jnp.dot(factor[0], coefs[...], preferred_element_type=F32)

    @pl.when(part == 1)
    def _():
        imag = jnp.dot(factor[0], coefs[...], preferred_element_type=F32)
        half_lanes = lanes // 2
        swapped = jnp.concatenate([imag[:, half_lanes:], imag[:, :half_lanes]], 1)
        sign = jnp.where(lax.broadcasted_iota(jnp.int32, (1, lanes), 1) < half_lanes, -1.0, 1.0)
        flipped = (real[...] + swapped * sign).T
        owners, each, _ = out.shape
        half = each // 2
        for owner in range(owners):
            for ri in range(2):
                at = ri * (lanes // 2) + owner * half
                out[owner, ri * half:ri * half + half, :] = flipped[at:at + half].astype(BF16)


def gradient(coefs, factor, owners):
    parts, rows, cap = factor.shape
    lanes = coefs.shape[1]
    return pl.pallas_call(
        gradient_kernel,
        grid=(parts,),
        in_specs=[pl.BlockSpec((cap, lanes), lambda i: (0, 0)), pl.BlockSpec((1, rows, cap), lambda i: (i, 0, 0))],
        out_specs=pl.BlockSpec((owners, lanes // owners, rows), lambda i: (0, 0, 0)),
        out_shape=jax.ShapeDtypeStruct((owners, lanes // owners, rows), BF16),
        scratch_shapes=[pltpu.VMEM((rows, lanes), F32)],
        compiler_params=pltpu.CompilerParams(vmem_limit_bytes=20 << 20),
        cost_estimate=pl.CostEstimate(flops=4 * cap * rows * lanes, bytes_accessed=cap * lanes * 2, transcendentals=0),
        name="gradient",
    )(coefs, *in_hbm(factor))


def time_kernel(mute, arrived, basis, out, spectra, ready, sems):
    rows, share, times = ready.shape
    depth = basis.shape[0]
    here = rows // sems.shape[0]
    spectra[...] = arrived[...].reshape(depth, rows).astype(F32).T
    lane = lax.broadcasted_iota(jnp.int32, (share, depth), 1)
    row = lax.broadcasted_iota(jnp.int32, (share, depth), 0)
    own = row == lane % share
    when = lax.broadcasted_iota(jnp.int32, (share, times), 1)

    def leaving(step):
        at = pl.ds(step * here, here)
        return pltpu.make_async_copy(ready.at[at], out.at[at], sems.at[step])

    def push(step, carry):
        base = step * here
        lines = []
        for n in range(here):
            lines.append(jnp.where(own, spectra[pl.ds(base + n, 1), :], 0.0).astype(BF16))
        got = jnp.dot(jnp.concatenate(lines, 0), basis[...], preferred_element_type=F32)
        signal = got[:, :times] + got[:, times:]
        for n in range(here):
            ready[base + n] = jnp.where(when >= mute[base + n], signal[n * share:n * share + share], 0.0).astype(BF16)
        leaving(step).start()
        return carry

    def finish(step, carry):
        leaving(step).wait()
        return carry

    for step in range(sems.shape[0]):
        push(step, 0)
    for step in range(sems.shape[0]):
        finish(step, 0)


def to_time(mute, arrived, basis, rows, share):
    vmem = pl.BlockSpec(memory_space=pltpu.VMEM)
    return pl.pallas_call(
        time_kernel,
        in_specs=[pl.BlockSpec(memory_space=pltpu.SMEM), vmem, vmem],
        out_specs=pl.BlockSpec(memory_space=pl.ANY),
        out_shape=jax.ShapeDtypeStruct((rows, share, NTIME), BF16),
        scratch_shapes=[
            pltpu.VMEM((rows, basis.shape[0]), F32),
            pltpu.VMEM((rows, share, NTIME), BF16),
            pltpu.SemaphoreType.DMA((TIME_PIECES,)),
        ],
        compiler_params=pltpu.CompilerParams(vmem_limit_bytes=16 << 20),
        name="to_time",
    )(mute, arrived, basis)


def shards(model_field, data_field, u_codes, u_scales, v_codes, v_scales, tile_ranks, mute_start):
    ranks = tile_ranks[0]
    tiles = ranks.shape[0]
    rows = model_field.shape[1]
    width = model_field.shape[2]
    freq_count = lax.axis_size("freq")
    sources = width // 2
    share = sources // freq_count
    basis = jnp.asarray(time_basis(freq_count, share))
    sent = coef(ranks, v_codes[0], v_scales[0], model_field[0])
    late_u, late_v, sent = lax.optimization_barrier((u_codes[0], v_codes[0], sent))
    arrived = lax.all_to_all(sent, "tile", split_axis=0, concat_axis=0, tiled=True)
    u_slots, u_turned = slots(True, True, ranks, late_u, u_scales[0])
    v_slots, = slots(False, False, ranks, late_v, v_scales[0])
    back = residual(arrived.reshape(tiles * RSLOT, width), u_slots, u_turned, data_field[0])
    back = lax.all_to_all(back.reshape(tiles, RSLOT, width), "tile", split_axis=0, concat_axis=0, tiled=True)
    part = gradient(back.reshape(tiles * RSLOT, width), v_slots, freq_count)
    spectra = lax.all_to_all(part, "freq", split_axis=0, concat_axis=0, tiled=True)
    return to_time(mute_start, spectra, basis, rows, share)


def solution(mesh):
    in_specs = (
        P("freq", "tile", None),
        P("freq", "tile", None),
        P("freq", None, "tile", None),
        P("freq", "tile", None),
        P("freq", None, "tile", None),
        P("freq", "tile", None),
        P("freq", None, None),
        P("tile"),
    )
    out_specs = P("tile", "freq", None)
    return jax.shard_map(shards, mesh=mesh, in_specs=in_specs, out_specs=out_specs, check_vma=False)
```

```python
import functools
import math

import jax
import jax.numpy as jnp
import numpy as np
from jax import lax
from jax.experimental import pallas as pl
from jax.experimental.pallas import tpu as pltpu
from jax.sharding import PartitionSpec as P

RSLOT = 88
NTIME = 128
BLK = 256
WIN = 384
STAGGER_NS = 17500
TIME_PIECES = 8
OUT_PIECES = 4
TURNED_SIXTEENTHS = (8,)
F32 = jnp.float32
BF16 = jnp.bfloat16
NT_DIMS = (((1,), (1,)), ((), ()))


def time_basis(freq_count, per):
    arg = 2.0 * math.pi * (np.arange(freq_count)[:, None] + 1.0) * np.arange(NTIME)[None, :] / NTIME
    base = 0.5 * np.stack([np.cos(arg), -np.sin(arg)], 1)
    rows = np.repeat(base.reshape(freq_count * 2, NTIME), per, 0).astype(np.float32)
    high = rows.astype(jnp.bfloat16)
    low = (rows - high.astype(np.float32)).astype(jnp.bfloat16)
    return np.concatenate([high, low], 1)


def start_all(*copies):
    for copy in copies:
        copy.start()
    return copies


def coef_kernel(ranks, codes, scale, model, out, plain, rotated, first, pool, ready, out_sems):
    part = pl.program_id(0)
    _, rows, cap = codes.shape
    tiles = ranks.shape[0]
    half = model.shape[1] // 2
    mine = lax.axis_index("tile")
    piece = cap // 2

    @pl.when(part == 0)
    def _():
        for lane in range(2):
            pool[lane, cap:cap + RSLOT + 8, :] = jnp.zeros((RSLOT + 8, 128), F32)
        turned = model[...].astype(F32).T
        plain[...] = turned.astype(BF16)
        rotated[:half] = turned[half:].astype(BF16)
        rotated[half:] = (-turned[:half]).astype(BF16)
        for at in range(0, cap, piece):
            first[:, at:at + piece] = jnp.dot(plain[...], codes[0, :, at:at + piece], preferred_element_type=F32)

    def move(tile, begin):
        for lane in range(2):
            ready[tile, :, lane * 128:lane * 128 + 128] = pool[lane, pl.ds(begin, RSLOT), :].astype(BF16)
        return begin + ranks[tile, mine]

    @pl.when(part == 1)
    def _():
        for at in range(0, cap, piece):
            acc = first[:, at:at + piece] + jnp.dot(rotated[...], codes[0, :, at:at + piece], preferred_element_type=F32)
            upright = (acc * scale[:, at:at + piece]).T
            for lane in range(2):
                pool[lane, at:at + piece, :] = upright[:, lane * 128:lane * 128 + 128]
        begin = jnp.int32(0)
        leaving = []
        per = tiles // OUT_PIECES
        for k in range(OUT_PIECES):
            begin = lax.fori_loop(k * per, k * per + per, move, begin)
            leaving.append(pltpu.make_async_copy(ready.at[pl.ds(k * per, per)], out.at[pl.ds(k * per, per)], out_sems.at[k]))
            leaving[-1].start()
        for copy in leaving:
            copy.wait()

        @pl.when(lax.axis_index("freq") % 2 == 1)
        def _():
            pl.delay(STAGGER_NS)


def in_hbm(*arrays):
    return [pltpu.with_memory_space_constraint(array, pltpu.HBM) for array in arrays]


def coef(ranks, codes, scale, model):
    parts, rows, cap = codes.shape
    width = model.shape[1]
    tiles = ranks.shape[0]
    return pl.pallas_call(
        coef_kernel,
        grid=(parts,),
        in_specs=[
            pl.BlockSpec(memory_space=pltpu.SMEM),
            pl.BlockSpec((1, rows, cap), lambda i: (i, 0, 0)),
            pl.BlockSpec(scale.shape, lambda i: (0, 0)),
            pl.BlockSpec(model.shape, lambda i: (0, 0)),
        ],
        out_specs=pl.BlockSpec(memory_space=pl.ANY),
        out_shape=jax.ShapeDtypeStruct((tiles, RSLOT, width), BF16),
        scratch_shapes=[
            pltpu.VMEM((width, rows), BF16),
            pltpu.VMEM((width, rows), BF16),
            pltpu.VMEM((width, cap), F32),
            pltpu.VMEM((2, cap + RSLOT + 8, 128), F32),
            pltpu.VMEM((tiles, RSLOT, width), BF16),
            pltpu.SemaphoreType.DMA((OUT_PIECES,)),
        ],
        compiler_params=pltpu.CompilerParams(vmem_limit_bytes=32 << 20),
        cost_estimate=pl.CostEstimate(flops=4 * cap * rows * width, bytes_accessed=parts * rows * cap * 2, transcendentals=0),
        name="coef",
    )(*in_hbm(ranks, codes, scale, model))


def slot_kernel(by_row, with_turned, ranks, codes, scale, *rest):
    out = rest[0]
    turned = rest[1] if with_turned else None
    begin, rank = rest[-2:]
    step = pl.program_id(0)
    tiles = ranks.shape[0]
    cap = codes.shape[2]
    mine = lax.axis_index("tile")

    @pl.when(step == 0)
    def _():
        def fill(tile, acc):
            here = ranks[mine, tile] if by_row else ranks[tile, mine]
            begin[tile] = acc
            rank[tile] = here
            return acc + here

        lax.fori_loop(0, tiles, fill, jnp.int32(0))

    first_tile = (step * BLK) // RSLOT
    inside = step * BLK - first_tile * RSLOT
    first = begin[first_tile] + jnp.minimum(inside, rank[first_tile])
    start = pl.multiple_of(jnp.minimum((first // 128) * 128, cap - WIN), 128)
    lane = lax.broadcasted_iota(jnp.int32, (1, BLK), 1)
    where_from = jnp.full((1, BLK), -1, jnp.int32)
    for ahead in range(-(-BLK // RSLOT) + 1):
        tile = jnp.minimum(first_tile + ahead, tiles - 1)
        offset = lane + (step * BLK - tile * RSLOT)
        live = (offset >= 0) & (offset < rank[tile])
        where_from = jnp.where(live, offset + (begin[tile] - start), where_from)
    picks = jnp.where(lax.broadcasted_iota(jnp.int32, (WIN, BLK), 0) == where_from, 1.0, 0.0).astype(BF16)
    window = scale[:, pl.ds(start, WIN)]
    high = window.astype(BF16).astype(F32)
    middle = (window - high).astype(BF16).astype(F32)
    low = window - high - middle
    row = lax.broadcasted_iota(jnp.int32, (16, WIN), 0)
    split = jnp.where(row == 0, high, jnp.where(row == 1, middle, jnp.where(row == 2, low, 0.0))).astype(BF16)
    weight = jnp.sum(jnp.dot(split, picks, preferred_element_type=F32), 0, keepdims=True)
    rows = codes.shape[1]
    for part in range(2):
        moved = jnp.dot(codes[part, :, pl.ds(start, WIN)], picks, preferred_element_type=F32) * weight
        out[part] = moved.astype(BF16)
        if with_turned:
            turned[:, part * rows:part * rows + rows] = moved.T.astype(BF16)


def slots(by_row, with_turned, ranks, codes, scale):
    parts, rows, cap = codes.shape
    tiles = ranks.shape[0]
    out_specs = [pl.BlockSpec((parts, rows, BLK), lambda i: (0, 0, i))]
    out_shape = [jax.ShapeDtypeStruct((parts, rows, tiles * RSLOT), BF16)]
    if with_turned:
        out_specs.append(pl.BlockSpec((BLK, parts * rows), lambda i: (i, 0)))
        out_shape.append(jax.ShapeDtypeStruct((tiles * RSLOT, parts * rows), BF16))
    return pl.pallas_call(
        functools.partial(slot_kernel, by_row, with_turned),
        grid=(tiles * RSLOT // BLK,),
        in_specs=[
            pl.BlockSpec(memory_space=pltpu.SMEM),
            pl.BlockSpec((parts, rows, cap), lambda i: (0, 0, 0), pipeline_mode=pl.Buffered(1)),
            pl.BlockSpec((1, cap), lambda i: (0, 0)),
        ],
        out_specs=out_specs,
        out_shape=out_shape,
        scratch_shapes=[pltpu.SMEM((tiles,), jnp.int32), pltpu.SMEM((tiles,), jnp.int32)],
        compiler_params=pltpu.CompilerParams(vmem_limit_bytes=16 << 20),
        cost_estimate=pl.CostEstimate(flops=4 * cap * rows * WIN, bytes_accessed=2 * parts * rows * cap * 2, transcendentals=0),
        name="slot_rows" if by_row else "slot_cols",
    )(ranks, codes, scale)


def complex_rows(stacked, rows, lanes):
    half = lanes // 2
    imag = stacked[rows:]
    swapped = jnp.concatenate([imag[:, half:], imag[:, :half]], 1)
    sign = jnp.where(lax.broadcasted_iota(jnp.int32, (1, lanes), 1) < half, -1.0, 1.0)
    return stacked[:rows] + swapped * sign


def piece_spans(total):
    spans, first = [], 0
    for part in TURNED_SIXTEENTHS:
        spans.append((first, total // 176 * 11 * part))
        first += spans[-1][1]
    return spans + [(first, total - first)]


def residual_kernel(coefs, factor, turned, data, out, held, real, both, ready, sems, out_sems):
    part = pl.program_id(0)
    _, rows, cap = factor.shape
    lanes = coefs.shape[1]
    half = lanes // 2
    spans = piece_spans(cap)
    copies = []
    for k, (first, size) in enumerate(spans):
        at = pl.ds(first, size)
        copies.append(pltpu.make_async_copy(turned.at[at], held.at[at], sems.at[k]))

    @pl.when(part == 0)
    def _():
        for copy in copies:
            copy.start()
        real[...] = jnp.dot(factor[0], coefs[...], preferred_element_type=F32)

    @pl.when(part == 1)
    def _():
        imag = jnp.dot(factor[0], coefs[...], preferred_element_type=F32)
        side = lax.broadcasted_iota(jnp.int32, (1, lanes), 1) < half
        swapped = jnp.concatenate([imag[:, half:], imag[:, :half]], 1)
        rest = (real[...] + swapped * jnp.where(side, -1.0, 1.0) - data[...].astype(F32)).astype(BF16).astype(F32)
        swapped = jnp.concatenate([rest[:, half:], rest[:, :half]], 1)
        both[:rows] = rest.astype(BF16)
        both[rows:] = (swapped * jnp.where(side, 1.0, -1.0)).astype(BF16)
        leaving = []
        weights = both[...]
        for k, (first, size) in enumerate(spans):
            copies[k].wait()
            at = slice(first, first + size)
            ready[at] = jnp.dot(held[at], weights, preferred_element_type=F32).astype(BF16)
            for part_of in range(2):
                at = slice(first + part_of * size // 2, first + (part_of + 1) * size // 2)
                leaving.append(pltpu.make_async_copy(ready.at[at], out.at[at], out_sems.at[2 * k + part_of]))
                leaving[-1].start()
        for copy in leaving:
            copy.wait()


def residual(coefs, factor, turned, data):
    parts, rows, cap = factor.shape
    lanes = coefs.shape[1]
    hbm = pl.BlockSpec(memory_space=pl.ANY)
    return pl.pallas_call(
        residual_kernel,
        grid=(parts,),
        in_specs=[
            pl.BlockSpec((cap, lanes), lambda i: (0, 0)),
            pl.BlockSpec((1, rows, cap), lambda i: (i, 0, 0)),
            hbm,
            pl.BlockSpec((rows, lanes), lambda i: (0, 0)),
        ],
        out_specs=hbm,
        out_shape=jax.ShapeDtypeStruct((cap, lanes), BF16),
        scratch_shapes=[
            pltpu.VMEM((cap, parts * rows), BF16),
            pltpu.VMEM((rows, lanes), F32),
            pltpu.VMEM((parts * rows, lanes), BF16),
            pltpu.VMEM((cap, lanes), BF16),
            pltpu.SemaphoreType.DMA((len(TURNED_SIXTEENTHS) + 1,)),
            pltpu.SemaphoreType.DMA((2 * len(TURNED_SIXTEENTHS) + 2,)),
        ],
        compiler_params=pltpu.CompilerParams(vmem_limit_bytes=32 << 20),
        cost_estimate=pl.CostEstimate(flops=8 * cap * rows * lanes, bytes_accessed=2 * cap * lanes * 2, transcendentals=0),
        name="residual",
    )(coefs, *in_hbm(factor, turned), data)


def gradient_kernel(coefs, factor, out, real):
    part = pl.program_id(0)
    _, rows, cap = factor.shape
    lanes = coefs.shape[1]

    @pl.when(part == 0)
    def _():
        real[...] = jnp.dot(factor[0], coefs[...], preferred_element_type=F32)

    @pl.when(part == 1)
    def _():
        imag = jnp.dot(factor[0], coefs[...], preferred_element_type=F32)
        half_lanes = lanes // 2
        swapped = jnp.concatenate([imag[:, half_lanes:], imag[:, :half_lanes]], 1)
        sign = jnp.where(lax.broadcasted_iota(jnp.int32, (1, lanes), 1) < half_lanes, -1.0, 1.0)
        flipped = (real[...] + swapped * sign).T
        owners, each, _ = out.shape
        half = each // 2
        for owner in range(owners):
            for ri in range(2):
                at = ri * (lanes // 2) + owner * half
                out[owner, ri * half:ri * half + half, :] = flipped[at:at + half].astype(BF16)


def gradient(coefs, factor, owners):
    parts, rows, cap = factor.shape
    lanes = coefs.shape[1]
    return pl.pallas_call(
        gradient_kernel,
        grid=(parts,),
        in_specs=[pl.BlockSpec((cap, lanes), lambda i: (0, 0)), pl.BlockSpec((1, rows, cap), lambda i: (i, 0, 0))],
        out_specs=pl.BlockSpec((owners, lanes // owners, rows), lambda i: (0, 0, 0)),
        out_shape=jax.ShapeDtypeStruct((owners, lanes // owners, rows), BF16),
        scratch_shapes=[pltpu.VMEM((rows, lanes), F32)],
        compiler_params=pltpu.CompilerParams(vmem_limit_bytes=20 << 20),
        cost_estimate=pl.CostEstimate(flops=4 * cap * rows * lanes, bytes_accessed=cap * lanes * 2, transcendentals=0),
        name="gradient",
    )(coefs, *in_hbm(factor))


def time_kernel(mute, arrived, basis, out, spectra, ready, sems):
    rows, share, times = ready.shape
    depth = basis.shape[0]
    here = rows // sems.shape[0]
    spectra[...] = arrived[...].reshape(depth, rows).astype(F32).T
    lane = lax.broadcasted_iota(jnp.int32, (share, depth), 1)
    row = lax.broadcasted_iota(jnp.int32, (share, depth), 0)
    own = row == lane % share
    when = lax.broadcasted_iota(jnp.int32, (share, times), 1)

    def leaving(step):
        at = pl.ds(step * here, here)
        return pltpu.make_async_copy(ready.at[at], out.at[at], sems.at[step])

    def push(step, carry):
        base = step * here
        lines = []
        for n in range(here):
            lines.append(jnp.where(own, spectra[pl.ds(base + n, 1), :], 0.0).astype(BF16))
        got = jnp.dot(jnp.concatenate(lines, 0), basis[...], preferred_element_type=F32)
        signal = got[:, :times] + got[:, times:]
        for n in range(here):
            ready[base + n] = jnp.where(when >= mute[base + n], signal[n * share:n * share + share], 0.0).astype(BF16)
        leaving(step).start()
        return carry

    def finish(step, carry):
        leaving(step).wait()
        return carry

    for step in range(sems.shape[0]):
        push(step, 0)
    for step in range(sems.shape[0]):
        finish(step, 0)


def to_time(mute, arrived, basis, rows, share):
    vmem = pl.BlockSpec(memory_space=pltpu.VMEM)
    return pl.pallas_call(
        time_kernel,
        in_specs=[pl.BlockSpec(memory_space=pltpu.SMEM), vmem, vmem],
        out_specs=pl.BlockSpec(memory_space=pl.ANY),
        out_shape=jax.ShapeDtypeStruct((rows, share, NTIME), BF16),
        scratch_shapes=[
            pltpu.VMEM((rows, basis.shape[0]), F32),
            pltpu.VMEM((rows, share, NTIME), BF16),
            pltpu.SemaphoreType.DMA((TIME_PIECES,)),
        ],
        compiler_params=pltpu.CompilerParams(vmem_limit_bytes=16 << 20),
        name="to_time",
    )(mute, arrived, basis)


def shards(model_field, data_field, u_codes, u_scales, v_codes, v_scales, tile_ranks, mute_start):
    ranks = tile_ranks[0]
    tiles = ranks.shape[0]
    rows = model_field.shape[1]
    width = model_field.shape[2]
    freq_count = lax.axis_size("freq")
    sources = width // 2
    share = sources // freq_count
    basis = jnp.asarray(time_basis(freq_count, share))
    sent = coef(ranks, v_codes[0], v_scales[0], model_field[0])
    late_u, late_v, sent = lax.optimization_barrier((u_codes[0], v_codes[0], sent))
    arrived = lax.all_to_all(sent, "tile", split_axis=0, concat_axis=0, tiled=True)
    u_slots, u_turned = slots(True, True, ranks, late_u, u_scales[0])
    v_slots, = slots(False, False, ranks, late_v, v_scales[0])
    back = residual(arrived.reshape(tiles * RSLOT, width), u_slots, u_turned, data_field[0])
    back = lax.all_to_all(back.reshape(tiles, RSLOT, width), "tile", split_axis=0, concat_axis=0, tiled=True)
    part = gradient(back.reshape(tiles * RSLOT, width), v_slots, freq_count)
    spectra = lax.all_to_all(part, "freq", split_axis=0, concat_axis=0, tiled=True)
    return to_time(mute_start, spectra, basis, rows, share)


def solution(mesh):
    in_specs = (
        P("freq", "tile", None),
        P("freq", "tile", None),
        P("freq", None, "tile", None),
        P("freq", "tile", None),
        P("freq", None, "tile", None),
        P("freq", "tile", None),
        P("freq", None, None),
        P("tile"),
    )
    out_specs = P("tile", "freq", None)
    return jax.shard_map(shards, mesh=mesh, in_specs=in_specs, out_specs=out_specs, check_vma=False)
```
